32 devices in a mesh: dp: 16 (over z, x, core), tensor: 2 (over y).
Axes of the slice: x: 2, y: 2, z: 4, core: 2. Of those that a mesh axis runs over, the one named last changes fastest.
Arguments:
- tokens: bfloat16 [37632, 768], P(('dp', 'tensor')), may hold values from -6 to 6
- cotangent: bfloat16 [37632, 768], P(('dp', 'tensor')), may hold values from -6 to 6
- window_extent: int32 [768, 2], P('dp'), may hold values from 1 to 7, as said below
- norm1_gain: float32 [768], replicated, may hold values from 0.25 to 1.75
- norm1_shift: float32 [768], replicated, may hold values from -1.25 to 1.25
- qkv_weight: bfloat16 [768, 3, 768], P(None, None, 'tensor'), may hold values from -0.21875 to 0.21875
- query_value_bias: float32 [2, 768], P(None, 'tensor'), may hold values from -1.75 to 1.75
- relative_bias: float32 [169, 24], P(None, 'tensor'), may hold values from -6 to 6
- proj_weight: bfloat16 [768, 768], P('tensor'), may hold values from -0.875 to 0.875
- proj_bias: float32 [768], replicated, may hold values from -1.75 to 1.75
- norm2_gain: float32 [768], replicated, may hold values from 0.25 to 1.75
- norm2_shift: float32 [768], replicated, may hold values from -1.25 to 1.25
- up_weight: bfloat16 [768, 3072], P(None, 'tensor'), may hold values from -0.21875 to 0.21875
- up_bias: float32 [3072], P('tensor'), may hold values from -1.75 to 1.75
- down_weight: bfloat16 [3072, 768], P('tensor'), may hold values from -0.15625 to 0.15625
- down_bias: float32 [768], replicated, may hold values from -1.75 to 1.75
Outputs:
- block_out: bfloat16 [37632, 768], P(('dp', 'tensor'))
- tokens_grad: float32 [37632, 768], P(('dp', 'tensor'))
- norm1_gain_grad: float32 [768], replicated
- norm1_shift_grad: float32 [768], replicated
- qkv_weight_grad: float32 [768, 3, 768], P(None, None, 'tensor')
- query_value_bias_grad: float32 [2, 768], P(None, 'tensor')
- relative_bias_grad: float32 [169, 24], P(None, 'tensor')
- proj_weight_grad: float32 [768, 768], P('tensor')
- proj_bias_grad: float32 [768], replicated
- norm2_gain_grad: float32 [768], replicated
- norm2_shift_grad: float32 [768], replicated
- up_weight_grad: float32 [768, 3072], P(None, 'tensor')
- up_bias_grad: float32 [3072], P('tensor')
- down_weight_grad: float32 [3072, 768], P('tensor')
- down_bias_grad: float32 [768], replicated
The draws below stay inside these ranges and needn't reach their ends.
Inputs may be any that keep to these rules, and one draw needn't show every extreme that they name: `window_extent`: windows come in aligned groups of four. A group holds either four images of 7 x 7 patches, each extent (7, 7), or the four windows of one image of 8 x 7 + 1 patches padded to 14 x 2 * 7, with extents (7, 7), (7, 1), (1, 7), (1, 1) in that order.
All inputs are finite; a program needn't handle non-finite values.
Results may differ from the reference program's by a relative error of at most 0.017.
Values may be sent and summed in bfloat16 or wider, within the bound.
No kernel may reach another device: no remote copies, remote signals or barrier semaphores. Data moves between devices by JAX's collectives and lax.ppermute only.
A program may use at most 192 MiB of HBM per device.

```python
import math
import jax
import jax.numpy as jnp
from jax import lax

D = 768
HEADS = 24
HEAD_DIM = 32
FF = 3072
WIN = 7
WIN_DEV = 48
REL = 169
WINDOWS = 768
TOKENS = 37632
N_DP = 16


def draw_window_extent(key, part):
    groups = WINDOWS // 4
    kinds = jax.random.randint(key, (groups,), 0, 2)
    kinds = kinds.at[0].set(1)
    drawn = jnp.full((4, 2), WIN, jnp.int32)
    padded = jnp.array([[WIN, WIN], [WIN, 1], [1, WIN], [1, 1]], jnp.int32)
    table = jnp.where(kinds[:, None, None] == 1, padded[None], drawn[None])
    return table.reshape(WINDOWS, 2).astype(jnp.int32)


def steps_of(own_key, extent, cuts, least, largest):
    level, own = 1.0, jax.random.fold_in(own_key, 6)
    for dim, blocks in cuts:
        draws = jnp.exp(jax.random.uniform(jax.random.fold_in(own, dim), (blocks,), jnp.float32, least / len(cuts), largest / len(cuts)))
        level = level * jnp.repeat(draws, extent[dim] // blocks).reshape([-1 if axis == dim else 1 for axis in range(len(extent))])
    return level


def scatter_about(key, shape, scale, reach, split=(), kind=jnp.bfloat16):
    loudness = steps_of(key, shape, split, -0.22, 0.18) if split else 1.0
    values = jax.random.normal(key, shape, jnp.float32) * scale * loudness
    return jnp.minimum(jnp.maximum(values, -reach), reach).astype(kind)


def setup_inputs(seed: int = 0) -> dict:
    arg_keys = jax.random.split(jax.random.key(seed), 17)
    tokens = scatter_about(arg_keys[0], (TOKENS, D), 1.0, 6.0, ((0, 32),))
    cotangent = scatter_about(arg_keys[1], (TOKENS, D), 1.0, 6.0, ((0, 32),))
    window_extent = draw_window_extent(jax.random.fold_in(arg_keys[16], 71), 0)
    norm1_gain = jnp.clip(1.0 + 0.15 * jax.random.normal(arg_keys[3], (D,), jnp.float32), 0.25, 1.75)
    norm1_shift = scatter_about(arg_keys[4], (D,), 0.2, 1.25, (), jnp.float32)
    qkv_weight = scatter_about(arg_keys[5], (D, 3, D), D ** -0.5, 0.21875, ((2, 2),))
    query_value_bias = scatter_about(arg_keys[6], (2, D), 0.3, 1.75, ((1, 2),), jnp.float32)
    relative_bias = scatter_about(arg_keys[7], (REL, HEADS), 1.0, 6.0, ((1, 2),), jnp.float32)
    proj_weight = scatter_about(arg_keys[8], (D, D), (D // 16) ** -0.5, 0.875, ((0, 2),))
    proj_bias = scatter_about(arg_keys[9], (D,), 0.3, 1.75, (), jnp.float32)
    norm2_gain = jnp.clip(1.0 + 0.15 * jax.random.normal(arg_keys[10], (D,), jnp.float32), 0.25, 1.75)
    norm2_shift = scatter_about(arg_keys[11], (D,), 0.2, 1.25, (), jnp.float32)
    up_weight = scatter_about(arg_keys[12], (D, FF), D ** -0.5, 0.21875, ((1, 2),))
    up_bias = scatter_about(arg_keys[13], (FF,), 0.3, 1.75, ((0, 2),), jnp.float32)
    down_weight = scatter_about(arg_keys[14], (FF, D), (FF // 2) ** -0.5, 0.15625, ((0, 2),))
    down_bias = scatter_about(arg_keys[15], (D,), 0.3, 1.75, (), jnp.float32)
    return dict(tokens=tokens, cotangent=cotangent, window_extent=window_extent, norm1_gain=norm1_gain, norm1_shift=norm1_shift, qkv_weight=qkv_weight, query_value_bias=query_value_bias, relative_bias=relative_bias, proj_weight=proj_weight, proj_bias=proj_bias, norm2_gain=norm2_gain, norm2_shift=norm2_shift, up_weight=up_weight, up_bias=up_bias, down_weight=down_weight, down_bias=down_bias)


@jax.custom_vjp
def low(v):
    return lax.optimization_barrier(v.astype(jnp.bfloat16)).astype(jnp.float32)

@jax.custom_vjp
def low_back(v):
    return v

def low_keep(v):
    return (low(v), None)

def low_pass(kept, grad):
    return (grad,)

def back_keep(v):
    return (v, None)

def back_low(kept, grad):
    return (low(grad),)
low.defvjp(low_keep, low_pass)
low_back.defvjp(back_keep, back_low)
norm_epsilon = 1e-05
masked_score = -1e+30

def matmul(left, right):
    return jnp.dot(left, right, precision=lax.Precision.HIGHEST, preferred_element_type=jnp.float32)

def layer_norm(values, gain, shift):
    center = values - lax.optimization_barrier(jnp.mean(values, axis=-1, keepdims=True))
    spread = lax.optimization_barrier(jnp.mean(center * center, axis=-1, keepdims=True))
    return center * lax.rsqrt(spread + norm_epsilon) * gain + shift

def window_masks(window_extent):
    places = jnp.arange(WIN * WIN, dtype=jnp.int32)
    rows_at = places // WIN
    cols_at = places % WIN
    return (rows_at[None, :] < window_extent[:, 0:1]) & (cols_at[None, :] < window_extent[:, 1:2])

def relative_index():
    places = jnp.arange(WIN * WIN, dtype=jnp.int32)
    rows_at = places // WIN
    cols_at = places % WIN
    return ((rows_at[:, None] - rows_at[None, :] + WIN - 1) * (2 * WIN - 1) + cols_at[:, None] - cols_at[None, :] + WIN - 1).astype(jnp.int32)

def attend_block(queries, key_rows, value_rows, key_mask, bias_full):
    scores = jnp.einsum('wihd,wjhd->whij', queries, key_rows, precision=lax.Precision.HIGHEST) * HEAD_DIM ** (-0.5)
    scores = low_back(scores + bias_full[None])
    scores = jnp.where(key_mask[:, None, None, :], scores, masked_score)
    probs = jax.nn.softmax(scores, axis=-1)
    return jnp.einsum('whij,wjhd->wihd', low(probs), value_rows, precision=lax.Precision.HIGHEST)

def block_forward(weights, tokens_group, key_mask):
    norm1_gain, norm1_shift, qkv_weight, query_value_bias, relative_bias, proj_weight, proj_bias, norm2_gain, norm2_shift, up_weight, up_bias, down_weight, down_bias = weights
    normed1 = low(layer_norm(tokens_group, norm1_gain, norm1_shift))
    mixed = matmul(normed1, qkv_weight.reshape(D, 3 * D)).reshape(-1, 3, D)
    queries = low(low_back(mixed[:, 0]) + query_value_bias[0])
    key_rows = low(low_back(mixed[:, 1]))
    value_rows = low(low_back(mixed[:, 2]) + query_value_bias[1])
    bias_full = jnp.transpose(relative_bias[relative_index()], (2, 0, 1))
    per_block = math.gcd(WIN_DEV, 12)
    count = WIN_DEV // per_block
    shape = (count, per_block, WIN * WIN, HEADS, HEAD_DIM)
    checked = jax.checkpoint(attend_block)

    def run_block(pieces):
        return checked(pieces[0], pieces[1], pieces[2], pieces[3], bias_full)
    attended = lax.map(run_block, (queries.reshape(shape), key_rows.reshape(shape), value_rows.reshape(shape), key_mask.reshape(count, per_block, WIN * WIN)))
    attended = low(low_back(attended.reshape(-1, D)))
    residual = tokens_group + low_back(matmul(attended, proj_weight)) + proj_bias
    normed2 = low(layer_norm(residual, norm2_gain, norm2_shift))
    hidden = low_back(matmul(normed2, up_weight)) + up_bias
    activation = low(jax.nn.gelu(hidden, approximate=False))
    down = low_back(matmul(activation, down_weight)) + down_bias
    valid = key_mask.reshape(-1, 1).astype(jnp.float32)
    return valid * (residual + down)

def reference(tokens, cotangent, window_extent, norm1_gain, norm1_shift, qkv_weight, query_value_bias, relative_bias, proj_weight, proj_bias, norm2_gain, norm2_shift, up_weight, up_bias, down_weight, down_bias):
    weights = tuple((item.astype(jnp.float32) for item in (norm1_gain, norm1_shift, qkv_weight, query_value_bias, relative_bias, proj_weight, proj_bias, norm2_gain, norm2_shift, up_weight, up_bias, down_weight, down_bias)))
    token_groups = tokens.astype(jnp.float32).reshape(N_DP, WIN_DEV * WIN * WIN, D)
    grad_groups = cotangent.astype(jnp.float32).reshape(N_DP, WIN_DEV * WIN * WIN, D)
    mask_groups = window_masks(window_extent).reshape(N_DP, WIN_DEV, WIN * WIN)

    def one_group(totals, pieces):
        tokens_in, grad_in, mask_in = pieces

        def forward(weights_in, values_in):
            return block_forward(weights_in, values_in, mask_in)
        result, pullback = jax.vjp(forward, weights, tokens_in)
        weight_grads, input_grad = pullback(grad_in)
        totals = jax.tree.map(lambda first, second: first + second, totals, weight_grads)
        return (totals, (result.astype(jnp.bfloat16), input_grad))
    zeros = jax.tree.map(jnp.zeros_like, weights)
    totals, (outputs, input_grads) = lax.scan(one_group, zeros, (token_groups, grad_groups, mask_groups))
    return (outputs.reshape(TOKENS, D), input_grads.reshape(TOKENS, D), totals[0], totals[1], totals[2], totals[3], totals[4], totals[5], totals[6], totals[7], totals[8], totals[9], totals[10], totals[11], totals[12])
```

```python
import functools
import jax, jax.numpy as jnp
from jax import lax
from jax.experimental import pallas as pl
from jax.experimental.pallas import tpu as pltpu
from jax.sharding import PartitionSpec as P

WIN = 7
PATCHES = WIN * WIN
SLOT = 64
LANES = 128
HEAD_DIM = 32
PER_GROUP = LANES // HEAD_DIM
SPREAD = PER_GROUP * SLOT
BLOCK = 8
ROWS = BLOCK * PATCHES
SCALE = HEAD_DIM ** -0.5


def dot_last(left, right):
    return lax.dot_general(left, right, (((1,), (1,)), ((), ())), preferred_element_type=jnp.float32)


def dot_first(left, right):
    return lax.dot_general(left, right, (((0,), (0,)), ((), ())), preferred_element_type=jnp.float32)


def dot_plain(left, right):
    return jnp.dot(left, right, preferred_element_type=jnp.float32)


def head_lanes(rows):
    lane = lax.broadcasted_iota(jnp.int32, (rows, LANES), 1) // HEAD_DIM
    return [lane == head for head in range(PER_GROUP)]


def spread_heads(rows, masks):
    zero = jnp.zeros_like(rows)
    return jnp.concatenate([jnp.where(mask, rows, zero) for mask in masks], axis=0)


def gather_heads(full, masks):
    out = jnp.zeros((SLOT, LANES), jnp.float32)
    for head, mask in enumerate(masks):
        out = jnp.where(mask, full[head * SLOT : (head + 1) * SLOT], out)
    return out


def attend_kernel(groups, x_ref, w_ref, shift_ref, bias_ref, mask_ref, att_ref, qkv_ref, prob_ref, mix, held, flat):
    width = groups * LANES
    mix[ROWS:, :] = jnp.zeros((mix.shape[0] - ROWS, 3 * width), jnp.float32)
    for part in range(3):
        cols = pl.ds(part * width, width)
        mix[:ROWS, cols] = dot_plain(x_ref[...], w_ref[:, cols]) + shift_ref[:, cols]
    for window in range(BLOCK):
        qkv_ref[window] = mix[pl.ds(window * PATCHES, SLOT), :].astype(jnp.bfloat16)
    masks = head_lanes(SLOT)
    low_half = lax.broadcasted_iota(jnp.int32, (SLOT, LANES), 1) < SLOT
    ones = (
        lax.broadcasted_iota(jnp.int32, (SPREAD, SPREAD), 0) // SLOT
        == lax.broadcasted_iota(jnp.int32, (SPREAD, SPREAD), 1) // SLOT
    ).astype(jnp.float32).astype(jnp.bfloat16)
    least = jnp.float32(-3e38)

    def segment_max(scores):
        parts = []
        for half in range(SPREAD // LANES):
            piece = scores[:, half * LANES : (half + 1) * LANES]
            first = jnp.max(jnp.where(low_half, piece, least), axis=-1, keepdims=True)
            second = jnp.max(jnp.where(low_half, least, piece), axis=-1, keepdims=True)
            parts.append(jnp.where(low_half, first, second))
        return jnp.concatenate(parts, axis=1)

    def one_window(window, carry):
        for group in range(groups):
            lanes = pl.ds(group * LANES, LANES)
            query = qkv_ref[window, :, lanes]
            key = spread_heads(qkv_ref[window, :, pl.ds(width + group * LANES, LANES)], masks)
            value = spread_heads(qkv_ref[window, :, pl.ds(2 * width + group * LANES, LANES)], masks)
            scores = dot_last(query, key) * SCALE + bias_ref[group] + mask_ref[window]
            weights = jnp.exp(scores - segment_max(scores))
            total = dot_plain(weights.astype(jnp.bfloat16), ones)
            probs = (weights / total).astype(jnp.bfloat16)
            prob_ref[window, group] = probs
            held[window, :, lanes] = dot_plain(probs, value)
        return carry

    lax.fori_loop(0, BLOCK, one_window, 0)
    for window in range(BLOCK):
        flat[pl.ds(window * PATCHES, SLOT), :] = held[window]
    att_ref[...] = flat[:ROWS, :].astype(jnp.bfloat16)


TAIL = (BLOCK - 1) * PATCHES + SLOT
TAIL = (TAIL + 7) // 8 * 8


def attend(normed, weight, shift, bias, mask):
    windows = mask.shape[0]
    width = weight.shape[1] // 3
    groups = width // LANES
    fixed = lambda shape: pl.BlockSpec(shape, lambda i: (0,) * len(shape))
    return pl.pallas_call(
        functools.partial(attend_kernel, groups),
        grid=(windows // BLOCK,),
        in_specs=[
            pl.BlockSpec((ROWS, normed.shape[1]), lambda i: (i, 0)),
            fixed(weight.shape),
            fixed(shift.shape),
            fixed(bias.shape),
            pl.BlockSpec((BLOCK, 1, SPREAD), lambda i: (i, 0, 0)),
        ],
        out_specs=[
            pl.BlockSpec((ROWS, width), lambda i: (i, 0)),
            pl.BlockSpec((BLOCK, SLOT, 3 * width), lambda i: (i, 0, 0)),
            pl.BlockSpec((BLOCK, groups, SLOT, SPREAD), lambda i: (i, 0, 0, 0)),
        ],
        out_shape=[
            jax.ShapeDtypeStruct((windows * PATCHES, width), jnp.bfloat16),
            jax.ShapeDtypeStruct((windows, SLOT, 3 * width), jnp.bfloat16),
            jax.ShapeDtypeStruct((windows, groups, SLOT, SPREAD), jnp.bfloat16),
        ],
        scratch_shapes=[
            pltpu.VMEM((TAIL, 3 * width), jnp.float32),
            pltpu.VMEM((BLOCK, SLOT, width), jnp.float32),
            pltpu.VMEM((TAIL, width), jnp.float32),
        ],
        cost_estimate=pl.CostEstimate(
            flops=2 * normed.size * weight.shape[1] + 8 * windows * groups * SLOT * SPREAD * SPREAD,
            bytes_accessed=2 * (normed.size + weight.size + windows * SLOT * (4 * width + groups * SPREAD)),
            transcendentals=windows * groups * SLOT * SPREAD,
        ),
    )(normed, weight, shift, bias, mask)


def attend_grad_kernel(groups, grad_ref, att_ref, qkv_ref, prob_ref, out_ref, table_ref, sum_ref, rise, pair, held, flat):
    width = groups * LANES
    step = pl.program_id(0)

    @pl.when(step == 0)
    def _():
        table_ref[...] = jnp.zeros_like(table_ref)
        sum_ref[...] = jnp.zeros_like(sum_ref)

    masks = head_lanes(SLOT)
    real = lax.broadcasted_iota(jnp.int32, (SLOT, LANES), 0) < PATCHES
    rise[ROWS:, :] = jnp.zeros((rise.shape[0] - ROWS, 2 * width), jnp.float32)
    for group in range(groups):
        lanes = pl.ds(group * LANES, LANES)
        grad = grad_ref[:, lanes].astype(jnp.float32)
        rise[:ROWS, pl.ds(2 * group * LANES, LANES)] = grad
        rise[:ROWS, pl.ds((2 * group + 1) * LANES, LANES)] = grad * att_ref[:, lanes].astype(jnp.float32)
    for window in range(BLOCK):
        for group in range(2 * groups):
            lanes = pl.ds(group * LANES, LANES)
            pair[window, :, lanes] = jnp.where(real, rise[pl.ds(window * PATCHES, SLOT), lanes], 0.0).astype(jnp.bfloat16)
    minus = spread_heads(jnp.full((SLOT, LANES), -1.0, jnp.bfloat16), masks)

    def one_window(window, carry):
        for group in range(groups):
            spot = [pl.ds(part * width + group * LANES, LANES) for part in range(3)]
            query = qkv_ref[window, :, spot[0]]
            key = spread_heads(qkv_ref[window, :, spot[1]], masks)
            value = spread_heads(qkv_ref[window, :, spot[2]], masks)
            both = pair[window, :, pl.ds(2 * group * LANES, 2 * LANES)]
            probs = prob_ref[window, group]
            lift = dot_last(both, jnp.concatenate([value, minus], axis=1))
            score_grad = (probs.astype(jnp.float32) * lift).astype(jnp.bfloat16)
            table_ref[group] += score_grad.astype(jnp.float32)
            held[window, :, spot[0]] = dot_plain(score_grad, key) * SCALE
            held[window, :, spot[1]] = gather_heads(dot_first(score_grad, query), masks) * SCALE
            held[window, :, spot[2]] = gather_heads(dot_first(probs, both[:, :LANES]), masks)
        return carry

    lax.fori_loop(0, BLOCK, one_window, 0)
    for window in range(BLOCK):
        flat[pl.ds(window * PATCHES, SLOT), :] = held[window]
    out_ref[...] = flat[:ROWS, :].astype(jnp.bfloat16)
    sum_ref[...] += jnp.sum(flat[:ROWS, :].reshape(ROWS // 8, 8, 3 * width), axis=0)


def attend_grad(grad, attended, qkv, probs):
    windows, groups = probs.shape[:2]
    width = groups * LANES
    rows = lambda cols: pl.BlockSpec((ROWS, cols), lambda i: (i, 0))
    return pl.pallas_call(
        functools.partial(attend_grad_kernel, groups),
        grid=(windows // BLOCK,),
        in_specs=[
            rows(width),
            rows(width),
            pl.BlockSpec((BLOCK, SLOT, 3 * width), lambda i: (i, 0, 0)),
            pl.BlockSpec((BLOCK, groups, SLOT, SPREAD), lambda i: (i, 0, 0, 0)),
        ],
        out_specs=[
            rows(3 * width),
            pl.BlockSpec((groups, SLOT, SPREAD), lambda i: (0, 0, 0)),
            pl.BlockSpec((8, 3 * width), lambda i: (0, 0)),
        ],
        out_shape=[
            jax.ShapeDtypeStruct((windows * PATCHES, 3 * width), jnp.bfloat16),
            jax.ShapeDtypeStruct((groups, SLOT, SPREAD), jnp.float32),
            jax.ShapeDtypeStruct((8, 3 * width), jnp.float32),
        ],
        scratch_shapes=[
            pltpu.VMEM((TAIL, 2 * width), jnp.float32),
            pltpu.VMEM((BLOCK, SLOT, 2 * width), jnp.bfloat16),
            pltpu.VMEM((BLOCK, SLOT, 3 * width), jnp.float32),
            pltpu.VMEM((TAIL, 3 * width), jnp.float32),
        ],
        cost_estimate=pl.CostEstimate(
            flops=16 * windows * groups * SLOT * SPREAD * SPREAD,
            bytes_accessed=2 * windows * SLOT * (8 * width + groups * SPREAD),
            transcendentals=0,
        ),
    )(grad, attended, qkv, probs)


norm_epsilon = 1e-05
masked_score = -1e30
highest = lax.Precision.HIGHEST
low = jnp.bfloat16


def window_masks(window_extent):
    places = jnp.arange(PATCHES, dtype=jnp.int32)
    rows_at = places // WIN
    cols_at = places % WIN
    return (rows_at[None, :] < window_extent[:, 0:1]) & (cols_at[None, :] < window_extent[:, 1:2])


def relative_onehot():
    places = jnp.arange(PATCHES, dtype=jnp.int32)
    rows_at = places // WIN
    cols_at = places % WIN
    index = (
        (rows_at[:, None] - rows_at[None, :] + WIN - 1) * (2 * WIN - 1)
        + cols_at[:, None]
        - cols_at[None, :]
        + WIN
        - 1
    )
    slots = jnp.arange((2 * WIN - 1) ** 2, dtype=jnp.int32)
    return (index.reshape(-1)[:, None] == slots[None, :]).astype(jnp.float32)


def spread_bias(onehot, table):
    heads = table.shape[1]
    flat = jnp.dot(onehot, table, precision=highest, preferred_element_type=jnp.float32)
    square = flat.T.reshape(heads, PATCHES, PATCHES)
    rest = SLOT - PATCHES
    square = jnp.pad(square, ((0, 0), (0, rest), (0, 0)))
    square = jnp.pad(square, ((0, 0), (0, 0), (0, rest)), constant_values=masked_score)
    square = square.reshape(heads // PER_GROUP, PER_GROUP, SLOT, SLOT)
    return square.transpose(0, 2, 1, 3).reshape(heads // PER_GROUP, SLOT, SPREAD)


def collect_bias(onehot, grads):
    groups = grads.shape[0]
    square = grads.reshape(groups, SLOT, PER_GROUP, SLOT)[:, :PATCHES, :, :PATCHES]
    square = square.transpose(0, 2, 1, 3).reshape(groups * PER_GROUP, PATCHES * PATCHES)
    return lax.dot_general(
        onehot, square, (((0,), (1,)), ((), ())), precision=highest, preferred_element_type=jnp.float32
    )


def norm_forward(values, gain, shift):
    center = values - jnp.mean(values, axis=-1, keepdims=True)
    inverse = lax.rsqrt(jnp.mean(center * center, axis=-1, keepdims=True) + norm_epsilon)
    unit = center * inverse
    return (unit * gain + shift, unit, inverse)


def norm_backward(normed_grad, unit, inverse, gain):
    unit_grad = normed_grad * gain
    inputs_grad = inverse * (
        unit_grad
        - jnp.mean(unit_grad, axis=-1, keepdims=True)
        - unit * jnp.mean(unit_grad * unit, axis=-1, keepdims=True)
    )
    return (inputs_grad, jnp.sum(normed_grad * unit, axis=0), jnp.sum(normed_grad, axis=0))


def gelu_parts(hidden):
    cdf = 0.5 * (1.0 + lax.erf(hidden * 0.7071067811865476))
    slope = cdf + hidden * jnp.exp(-0.5 * hidden * hidden) * 0.3989422804014327
    return (hidden * cdf, slope)


def add_low(first, second):
    return (first.astype(jnp.float32) + second.astype(jnp.float32)).astype(low)


class Links:
    def __init__(self):
        self.count = lax.axis_size("dp")
        self.me = lax.axis_index("dp")
        self.rest = []
        bit = 4
        while bit < self.count:
            self.rest.append(bit)
            bit *= 2

    def hop(self, values, bit):
        return lax.ppermute(values, "dp", [(i, i ^ bit) for i in range(self.count)])

    def across(self, values):
        return lax.ppermute(values, "tensor", [(0, 1), (1, 0)])

    def side(self, bit):
        return (self.me // bit) % 2

    def fetch(self, weight):
        part = weight.shape[0] // 4
        place = lambda bit: ((self.me % 4) ^ bit) * part
        mine = lax.dynamic_slice_in_dim(weight, place(0), part, 0)
        first = self.across(mine)
        second = self.hop(first, 2)
        out = jnp.zeros_like(weight)
        pieces = ((first, 0), (second, 2), (self.hop(first, 1), 1), (self.hop(second, 1), 3))
        for piece, bit in pieces:
            out = lax.dynamic_update_slice_in_dim(out, piece, place(bit), 0)
        return out

    def halve(self, values, bit):
        part = values.shape[0] // 2
        side = self.side(bit)
        keep = lax.dynamic_slice_in_dim(values, side * part, part, 0)
        give = lax.dynamic_slice_in_dim(values, (1 - side) * part, part, 0)
        return add_low(keep, self.hop(give, bit))

    def join(self, values, bit):
        other = self.hop(values, bit)
        first = self.side(bit) == 0
        return jnp.concatenate([jnp.where(first, values, other), jnp.where(first, other, values)], axis=0)

    def share(self, other):
        return self.across(self.halve(other, 1))

    def reduce(self, own, arrived):
        values = self.halve(add_low(self.halve(own, 1), arrived), 2)
        for bit in self.rest:
            values = self.halve(values, bit)
        for bit in reversed(self.rest):
            values = self.join(values, bit)
        part = values.shape[0]
        place = lambda core, line: ((self.side(1) ^ core) * 2 + (self.side(2) ^ line)) * part
        second = self.hop(values, 2)
        out = jnp.zeros(own.shape, jnp.float32)
        pieces = ((values, 0, 0), (second, 0, 1), (self.hop(values, 1), 1, 0), (self.hop(second, 1), 1, 1))
        for piece, core, line in pieces:
            out = lax.dynamic_update_slice_in_dim(out, piece.astype(jnp.float32), place(core, line), 0)
        return out

    def total(self, values):
        for bit in [1, 2] + self.rest:
            values = values + self.hop(values, bit)
        return values


def pack(items):
    flat = jnp.concatenate([item.reshape(-1) for item in items])
    return jnp.pad(flat, (0, -flat.shape[0] % 1024)).reshape(-1, LANES)


def unpack(packed, shapes):
    flat, items, start = packed.reshape(-1), [], 0
    for shape in shapes:
        size = 1
        for extent in shape:
            size *= extent
        items.append(flat[start : start + size].reshape(shape))
        start += size
    return items


def local(
    tokens,
    cotangent,
    window_extent,
    norm1_gain,
    norm1_shift,
    qkv_weight,
    query_value_bias,
    relative_bias,
    proj_weight,
    proj_bias,
    norm2_gain,
    norm2_shift,
    up_weight,
    up_bias,
    down_weight,
    down_bias,
):
    width = tokens.shape[1]
    links = Links()
    key_mask = window_masks(window_extent)
    own_windows = key_mask.shape[0] // lax.axis_size("tensor")
    own_mask = lax.dynamic_slice_in_dim(
        key_mask, lax.axis_index("tensor") * own_windows, own_windows, 0
    )
    row_mask = own_mask.reshape(-1, 1).astype(jnp.float32)
    lane_mask = jnp.pad(own_mask, ((0, 0), (0, SLOT - PATCHES)), constant_values=True)
    lane_mask = jnp.where(jnp.tile(lane_mask, (1, PER_GROUP)), 0.0, masked_score)[:, None, :]
    onehot = relative_onehot()
    part_width = qkv_weight.shape[2]
    small_shapes = [query_value_bias.shape, relative_bias.shape, up_bias.shape]
    own_small = [query_value_bias, relative_bias, up_bias]
    other_small = unpack(links.across(pack(own_small)), small_shapes)
    qkv_own = qkv_weight.reshape(width, 3 * part_width)
    qkv_both = [qkv_own, links.fetch(qkv_own)]
    proj_both = [proj_weight, links.fetch(proj_weight)]
    up_both = [up_weight, links.fetch(up_weight)]
    down_both = [down_weight, links.fetch(down_weight)]
    shift_both, bias_both, up_bias_both = [], [], []
    for pair_bias, table, hidden_bias in (own_small, other_small):
        shift = jnp.concatenate([pair_bias[0], jnp.zeros_like(pair_bias[0]), pair_bias[1]])
        shift_both.append(shift[None])
        bias_both.append(spread_bias(onehot, table))
        up_bias_both.append(hidden_bias)

    inputs = tokens.astype(jnp.float32)
    normed1, unit1, inverse1 = norm_forward(inputs, norm1_gain, norm1_shift)
    normed1_low = normed1.astype(low)
    heads = [
        attend(normed1_low, qkv_both[side], shift_both[side], bias_both[side], lane_mask)
        for side in (0, 1)
    ]
    branch = dot_plain(heads[0][0], proj_both[0]) + dot_plain(heads[1][0], proj_both[1])
    residual = inputs + branch + proj_bias
    normed2, unit2, inverse2 = norm_forward(residual, norm2_gain, norm2_shift)
    normed2_low = normed2.astype(low)
    activations, slopes = [], []
    for side in (0, 1):
        activation, slope = gelu_parts(dot_plain(normed2_low, up_both[side]) + up_bias_both[side])
        activations.append(activation.astype(low))
        slopes.append(slope)
    down = dot_plain(activations[0], down_both[0]) + dot_plain(activations[1], down_both[1])
    block_out = (row_mask * (residual + down + down_bias)).astype(low)

    out_grad = row_mask * cotangent.astype(jnp.float32)
    down_bias_grad = jnp.sum(out_grad, axis=0)
    out_low = out_grad.astype(low)
    shared = {}
    down_grads, up_grads, up_bias_grads, hidden_lows = {}, {}, {}, {}
    for side in (1, 0):
        down_grads[side] = dot_first(activations[side], out_low).astype(low)
        hidden_grad = dot_last(out_low, down_both[side]) * slopes[side]
        up_bias_grads[side] = jnp.sum(hidden_grad, axis=0)
        hidden_lows[side] = hidden_grad.astype(low)
        up_grads[side] = dot_first(normed2_low, hidden_lows[side]).astype(low)
        if side == 1:
            shared["down"] = links.share(down_grads[1])
            shared["up"] = links.share(up_grads[1])
    down_weight_grad = links.reduce(down_grads[0], shared["down"])
    up_weight_grad = links.reduce(up_grads[0], shared["up"])
    normed2_grad = dot_last(hidden_lows[0], up_both[0]) + dot_last(hidden_lows[1], up_both[1])
    residual_part, norm2_gain_grad, norm2_shift_grad = norm_backward(
        normed2_grad, unit2, inverse2, norm2_gain
    )
    residual_grad = out_grad + residual_part
    proj_bias_grad = jnp.sum(residual_grad, axis=0)
    residual_low = residual_grad.astype(low)
    proj_grads = [dot_first(heads[side][0], residual_low).astype(low) for side in (0, 1)]
    proj_weight_grad = links.reduce(proj_grads[0], links.share(proj_grads[1]))
    mixed_grads, table_grads, pair_grads, qkv_grads = {}, {}, {}, {}
    for side in (1, 0):
        attended_grad = dot_last(residual_low, proj_both[side]).astype(low)
        attended, qkv, probs = heads[side]
        mixed_grads[side], table, sums = attend_grad(attended_grad, attended, qkv, probs)
        table_grads[side] = collect_bias(onehot, table)
        sums = jnp.sum(sums, axis=0).reshape(3, part_width)
        pair_grads[side] = jnp.stack([sums[0], sums[2]])
        qkv_grads[side] = dot_first(normed1_low, mixed_grads[side]).astype(low)
        if side == 1:
            shared["qkv"] = links.share(qkv_grads[1])
    qkv_weight_grad = links.reduce(qkv_grads[0], shared["qkv"]).reshape(width, 3, part_width)
    normed1_grad = dot_last(mixed_grads[0], qkv_both[0]) + dot_last(mixed_grads[1], qkv_both[1])
    tokens_part, norm1_gain_grad, norm1_shift_grad = norm_backward(
        normed1_grad, unit1, inverse1, norm1_gain
    )
    tokens_grad = residual_grad + tokens_part

    everywhere = [
        norm1_gain_grad,
        norm1_shift_grad,
        proj_bias_grad,
        norm2_gain_grad,
        norm2_shift_grad,
        down_bias_grad,
    ]
    own_part = pack([pair_grads[0], table_grads[0], up_bias_grads[0]])
    other_part = pack([pair_grads[1], table_grads[1], up_bias_grads[1]])
    both_part = pack(everywhere)
    arrived = links.across(jnp.concatenate([other_part, both_part], axis=0))
    sums = links.total(jnp.concatenate([own_part, both_part], axis=0) + arrived)
    query_value_bias_grad, relative_bias_grad, up_bias_grad = unpack(
        sums[: own_part.shape[0]], small_shapes
    )
    everywhere = unpack(sums[own_part.shape[0] :], [(width,)] * len(everywhere))
    (
        norm1_gain_grad,
        norm1_shift_grad,
        proj_bias_grad,
        norm2_gain_grad,
        norm2_shift_grad,
        down_bias_grad,
    ) = everywhere
    return (
        block_out,
        tokens_grad,
        norm1_gain_grad,
        norm1_shift_grad,
        qkv_weight_grad,
        query_value_bias_grad,
        relative_bias_grad,
        proj_weight_grad,
        proj_bias_grad,
        norm2_gain_grad,
        norm2_shift_grad,
        up_weight_grad,
        up_bias_grad,
        down_weight_grad,
        down_bias_grad,
    )


def solution(mesh):
    return jax.shard_map(
        local,
        mesh=mesh,
        in_specs=(
            P(("dp", "tensor"), None),
            P(("dp", "tensor"), None),
            P("dp", None),
            P(),
            P(),
            P(None, None, "tensor"),
            P(None, "tensor"),
            P(None, "tensor"),
            P("tensor", None),
            P(),
            P(),
            P(),
            P(None, "tensor"),
            P("tensor"),
            P("tensor", None),
            P(),
        ),
        out_specs=(
            P(("dp", "tensor"), None),
            P(("dp", "tensor"), None),
            P(),
            P(),
            P(None, None, "tensor"),
            P(None, "tensor"),
            P(None, "tensor"),
            P("tensor", None),
            P(),
            P(),
            P(),
            P(None, "tensor"),
            P("tensor"),
            P("tensor", None),
            P(),
        ),
        check_vma=False,
    )
```
